32 devices in a mesh: ch: 4 (over y, x), row: 8 (over z, core).
Axes of the slice: x: 2, y: 2, z: 4, core: 2. Of those that a mesh axis runs over, the one named last changes fastest.
Arguments:
- latent: bfloat16 [128, 32, 1280], P('row', None, 'ch'), may hold values from -50 to 50
- timestep: int32 [4], replicated, may hold values from 0 to 999
- norm_gain_a: float32 [1280], P('ch'), may hold values from 0.1 to 1.9
- conv_weight_a: bfloat16 [1280, 3, 3, 1280], P('ch'), may hold values from -0.0546875 to 0.0546875
- time_weight: bfloat16 [320, 1280], P(None, 'ch'), may hold values from -0.3125 to 0.3125
- norm_gain_b: float32 [1280], P('ch'), may hold values from 0.1 to 1.9
- conv_weight_b: bfloat16 [1280, 3, 3, 1280], P('ch'), may hold values from -0.0546875 to 0.0546875
- norm_gain_c: float32 [1280], P('ch'), may hold values from 0.1 to 1.9
- w_query: bfloat16 [1024, 1280], P('ch'), may hold values from -4 to 4
- w_key: bfloat16 [1024, 1280], P('ch'), may hold values from -4 to 4
- w_value: bfloat16 [1024, 1280], P('ch'), may hold values from -0.3125 to 0.3125
- w_out: bfloat16 [1280, 1024], P('ch'), may hold values from -0.1875 to 0.1875
Outputs:
- result: bfloat16 [128, 32, 1280], P('row', None, 'ch')
The draws below stay inside these ranges and needn't reach their ends.
All inputs are finite; a program needn't handle non-finite values.
Results may differ from the reference program's by a relative error of at most 0.017.
Values may be sent and summed in bfloat16 or wider, within the bound.
A program may use at most 64 MiB of HBM per device.

```python
import math
import jax
import jax.numpy as jnp
from jax import lax

C = 1280
GROUPS = 32
HEAD_DIM = 64
TDIM = 320
HEADS = 16
H = 32
W = 32
IMGS = 4
ROWS = 128


def draw_latent(key, part):
    first, second, third = jax.random.split(key, 3)
    row_place = (jnp.arange(ROWS) % H).astype(jnp.float32)
    rising = 0.6 * (1.0 + 2.0 * row_place / (H - 1))
    row_scale = rising * jnp.exp(jax.random.uniform(first, (ROWS,), minval=-0.22, maxval=0.22))
    chan_scale = jnp.exp(jax.random.uniform(second, (C,), minval=math.log(0.3), maxval=math.log(3.0)))
    base = jax.random.truncated_normal(third, -4.0, 4.0, (ROWS, W, C))
    value = base * row_scale[:, None, None] * chan_scale[None, None, :]
    return jnp.clip(value, -50.0, 50.0).astype(jnp.bfloat16)


def projection_base(key, salt):
    return jax.random.normal(jax.random.fold_in(key, salt), (HEADS * HEAD_DIM, C)) / math.sqrt(C)


def draw_w_query(key, part):
    return jnp.clip(projection_base(key, 11), -4.0, 4.0).astype(jnp.bfloat16)


def draw_w_key(key, part):
    strength = jnp.exp(jax.random.uniform(jax.random.fold_in(key, 14), (HEADS,), minval=math.log(3.0), maxval=math.log(8.0)))
    value = jnp.repeat(strength, HEAD_DIM)[:, None] * projection_base(key, 12)
    return jnp.clip(value, -4.0, 4.0).astype(jnp.bfloat16)


def plant(array, key, least, top_value):
    longest = array.shape.index(max(array.shape))
    spots = []
    for shift in (0, 1):
        where = [jax.random.randint(jax.random.fold_in(key, axis), (), 0, length) for axis, length in enumerate(array.shape)]
        where[longest] = (where[longest] + shift) % array.shape[longest]
        spots.append(tuple(where))
    return array.at[spots[0]].set(least).at[spots[1]].set(top_value)


def level_of(rng, shape, cuts, least, top_value):
    level = 1.0
    for axis_at, blocks in cuts:
        draws = jax.random.uniform(jax.random.fold_in(jax.random.fold_in(rng, 6), axis_at), (blocks,), jnp.float32, least / len(cuts), top_value / len(cuts))
        level = level * jnp.repeat(jnp.exp(draws), shape[axis_at] // blocks).reshape((-1,) + (1,) * (len(shape) - 1 - axis_at))
    return level


def scatter_about(own_key, shape, deviation, limit, shards=(), kind=jnp.bfloat16):
    level = level_of(own_key, shape, shards, -0.22, 0.18) if shards else 1.0
    array = jax.random.normal(own_key, shape, jnp.float32) * deviation * level
    return jnp.minimum(jnp.maximum(array, -limit), limit).astype(kind)


def setup_inputs(seed: int = 0) -> dict:
    seeds = jax.random.split(jax.random.key(seed), 13)
    return {
        "latent": draw_latent(jax.random.fold_in(seeds[12], 71), 0),
        "timestep": plant(jax.random.randint(seeds[1], (IMGS,), 0, 1000), jax.random.fold_in(seeds[1], 1), 0, 999).astype(jnp.int32),
        "norm_gain_a": jnp.clip(1.0 + 0.18 * jax.random.normal(seeds[2], (C,), jnp.float32), 0.1, 1.9),
        "conv_weight_a": scatter_about(seeds[3], (C, 3, 3, C), (9 * C) ** -0.5, 0.0546875, ((0, 4),)),
        "time_weight": scatter_about(seeds[4], (TDIM, C), TDIM ** -0.5, 0.3125, ((1, 4),)),
        "norm_gain_b": jnp.clip(1.0 + 0.18 * jax.random.normal(seeds[5], (C,), jnp.float32), 0.1, 1.9),
        "conv_weight_b": scatter_about(seeds[6], (C, 3, 3, C), (9 * C) ** -0.5, 0.0546875, ((0, 4),)),
        "norm_gain_c": jnp.clip(1.0 + 0.18 * jax.random.normal(seeds[7], (C,), jnp.float32), 0.1, 1.9),
        "w_query": draw_w_query(jax.random.fold_in(seeds[12], 71), 0),
        "w_key": draw_w_key(jax.random.fold_in(seeds[12], 71), 0),
        "w_value": scatter_about(seeds[10], (HEADS * HEAD_DIM, C), (C // 4) ** -0.5, 0.3125, ((0, 4),)),
        "w_out": scatter_about(seeds[11], (C, HEADS * HEAD_DIM), (HEADS * HEAD_DIM) ** -0.5, 0.1875, ((0, 4),)),
    }


eps_value = 1e-06

def group_norm(value, gain):
    members = float(H * W * (C // GROUPS))
    flat = value.reshape(value.shape[0], H * W, GROUPS, C // GROUPS)
    mean = lax.optimization_barrier(jnp.sum(flat, axis=(1, 3))) / members
    spread = lax.optimization_barrier(jnp.sum(flat * flat, axis=(1, 3))) / members - mean * mean
    scaled = (flat - mean[:, None, :, None]) * lax.rsqrt(spread + eps_value)[:, None, :, None]
    return scaled.reshape(value.shape) * gain

def convolve(active, weight):
    kernel = jnp.transpose(weight, (1, 2, 3, 0))
    return lax.conv_general_dilated(active, kernel, (1, 1), 'SAME', dimension_numbers=('NHWC', 'HWIO', 'NHWC'), preferred_element_type=jnp.float32)

def right_product(left, weight):
    return lax.dot_general(left, weight, (((1,), (1,)), ((), ())), preferred_element_type=jnp.float32)

def reference(latent, timestep, norm_gain_a, conv_weight_a, time_weight, norm_gain_b, conv_weight_b, norm_gain_c, w_query, w_key, w_value, w_out):
    source = latent.reshape(IMGS, H, W, C).astype(jnp.float32)
    active_a = jax.nn.silu(group_norm(source, norm_gain_a)).astype(jnp.bfloat16)
    half = TDIM // 2
    freqs = jnp.exp(-math.log(10000.0) * jnp.arange(half, dtype=jnp.float32) / half)
    angles = timestep.astype(jnp.float32)[:, None] * freqs[None, :]
    sinus = jnp.concatenate([jnp.cos(angles), jnp.sin(angles)], axis=1).astype(jnp.bfloat16)
    time_add = jax.nn.silu(jnp.dot(sinus, time_weight, preferred_element_type=jnp.float32))
    hidden_a = convolve(active_a, conv_weight_a) + time_add[:, None, None, :]
    active_b = jax.nn.silu(group_norm(hidden_a, norm_gain_b)).astype(jnp.bfloat16)
    hidden_b = source + convolve(active_b, conv_weight_b)
    normed = group_norm(hidden_b, norm_gain_c).astype(jnp.bfloat16).reshape(IMGS, H * W, C)
    scale = 1.0 / math.sqrt(HEAD_DIM)

    def attend(tokens_in):
        query = right_product(tokens_in, w_query).astype(jnp.bfloat16)
        keyed = right_product(tokens_in, w_key).astype(jnp.bfloat16)
        valued = right_product(tokens_in, w_value).astype(jnp.bfloat16)
        query, keyed, valued = lax.optimization_barrier((query, keyed, valued))
        query_heads = query.astype(jnp.float32).reshape(H * W, HEADS, HEAD_DIM)
        key_heads = keyed.astype(jnp.float32).reshape(H * W, HEADS, HEAD_DIM)
        value_heads = valued.astype(jnp.float32).reshape(H * W, HEADS, HEAD_DIM)
        scores = jnp.einsum('qhd,khd->hqk', query_heads, key_heads) * scale
        weights = jax.nn.softmax(scores, axis=-1).astype(jnp.bfloat16)
        weights = lax.optimization_barrier(weights)
        heads_out = jnp.einsum('hqk,khd->qhd', weights.astype(jnp.float32), value_heads)
        return heads_out.astype(jnp.bfloat16).reshape(H * W, HEADS * HEAD_DIM)
    heads_out = lax.map(attend, normed).reshape(IMGS * H * W, HEADS * HEAD_DIM)
    projected = right_product(heads_out, w_out)
    total = hidden_b.reshape(IMGS * H * W, C) + projected
    return total.reshape(ROWS, W, C).astype(jnp.bfloat16)
```

```python
import functools
import math

import jax
import jax.numpy as jnp
from jax import lax
from jax.experimental import pallas as pl
from jax.experimental.pallas import tpu as pltpu
from jax.sharding import PartitionSpec as P

C = 1280
GROUPS = 32
HEAD_DIM = 64
TDIM = 320
H = 32


eps_value = 1e-06
MESH = pl.DeviceIdType.MESH


def swapped(value, axis, stride):
    mask = 2**stride
    pairs = [(source, source ^ mask) for source in range(lax.axis_size(axis))]
    return lax.ppermute(value, axis, pairs)


def right_product(left, weight):
    return lax.dot_general(
        left, weight, (((1,), (1,)), ((), ())), preferred_element_type=jnp.float32
    )


def flipped(place, bit):
    return place + bit * (1 - 2 * ((place // bit) % 2))


def combined(place, other, steps):
    total = 0
    for step in range(steps):
        bit = 2**step
        total = total + bit * (((place // bit) + (other // bit)) % 2)
    return total


def norm_kernel(active, block, group_width, members, *refs):
    value_ref, near, far, gain = refs[:4]
    outs = refs[4:]
    tokens, chunk = value_ref.shape
    main = outs[0].shape[1]

    lane_group = lax.broadcasted_iota(jnp.int32, (chunk, chunk), 1) // group_width
    depth_group = lax.broadcasted_iota(jnp.int32, (chunk, chunk), 0) // group_width
    same = jnp.where(lane_group == depth_group, 1.0, 0.0)
    stats = jnp.dot(
        near[...] + far[...], same, precision=lax.Precision.HIGHEST, preferred_element_type=jnp.float32
    )
    mean = stats[0:1] / members
    spread = stats[1:2] / members - mean * mean
    factor = lax.rsqrt(spread + eps_value)
    gains = gain[...]

    def scaled(span):
        value = value_ref[span, :].astype(jnp.float32)
        value = (value - mean) * factor * gains
        if active:
            value = jax.nn.silu(value)
        return value.astype(jnp.bfloat16)

    for step in range(tokens // (2 * block)):
        first = slice(step * block, (step + 1) * block)
        second = slice(tokens // 2 + step * block, tokens // 2 + (step + 1) * block)
        early, late = scaled(first), scaled(second)
        outs[0][first, :] = early[:, :main]
        outs[0][second, :] = late[:, :main]
        if len(outs) > 1:
            outs[1][first, :] = jnp.concatenate([early[:, main:], late[:, main:]], axis=1)


def normalized(value, near, far, gain, active, group_width, members):
    tokens, chunk = value.shape
    tail = chunk % 128 == 64 and chunk > 128
    vmem = pl.BlockSpec(memory_space=pltpu.VMEM)
    shapes = [jax.ShapeDtypeStruct((tokens, chunk - (64 if tail else 0)), jnp.bfloat16)]
    if tail:
        shapes = shapes + [jax.ShapeDtypeStruct((tokens // 2, 128), jnp.bfloat16)]
    return pl.pallas_call(
        functools.partial(norm_kernel, active, 64, group_width, members),
        out_shape=tuple(shapes),
        in_specs=[vmem] * 4,
        out_specs=tuple([vmem] * len(shapes)),
        compiler_params=pltpu.CompilerParams(vmem_limit_bytes=10 * 2**20),
    )(value, near, far, gain[None])


def gather_kernel(count, width, rim, kinds, *refs):
    owns, refs = refs[:kinds], refs[kinds:]
    full, refs = refs[0], refs[1:]
    slots, refs = refs[:kinds], refs[kinds:]
    if rim:
        edges, refs = refs[:kinds], refs[kinds:]
        send_sem, recv_sem, edge_send, edge_recv = refs
    else:
        send_sem, recv_sem = refs
    place = lax.axis_index("ch")
    row = lax.axis_index("row")
    steps = count.bit_length() - 1
    tokens = owns[0].shape[0]
    main = owns[0].shape[1]
    chunk = full.shape[1] // count
    partner = {"row": flipped(row, 1)}
    upper = 1 - row % 2

    barrier = pltpu.get_barrier_semaphore()
    for step in range(steps):
        pl.semaphore_signal(barrier, inc=1, device_id={"ch": flipped(place, 2**step)}, device_id_type=MESH)
    if rim:
        pl.semaphore_signal(barrier, inc=1, device_id=partner, device_id_type=MESH)
    pl.semaphore_wait(barrier, steps + (1 if rim else 0))

    orders = (list(range(steps)), list(range(steps))[::-1])

    def hops(relative, half, step):
        bit = 2 ** orders[half][step]
        target = relative ^ bit
        copies = []
        for kind in range(kinds):
            part = owns[kind].shape[0] // 2
            span = pl.ds(half * part, part)
            source = owns[kind].at[span] if relative == 0 else slots[kind].at[relative, span]
            copy = pltpu.make_async_remote_copy(
                src_ref=source,
                dst_ref=slots[kind].at[target, span],
                send_sem=send_sem.at[kind, target, half],
                recv_sem=recv_sem.at[kind, target, half],
                device_id={"ch": flipped(place, bit)},
                device_id_type=MESH,
            )
            copy.start()
            copies.append(copy)
        return copies

    def edge_hops(relative):
        copies = []
        for kind in range(kinds):
            begin = pl.multiple_of(upper * (owns[kind].shape[0] - width), width)
            span = pl.ds(begin, width)
            source = owns[kind].at[span] if relative == 0 else slots[kind].at[relative, span]
            copy = pltpu.make_async_remote_copy(
                src_ref=source,
                dst_ref=edges[kind].at[relative],
                send_sem=edge_send.at[kind, relative],
                recv_sem=edge_recv.at[kind, relative],
                device_id=partner,
                device_id_type=MESH,
            )
            copy.start()
            copies.append(copy)
        return copies

    def reached(half, step):
        found = [0]
        for earlier in range(step):
            found = found + [value ^ 2 ** orders[half][earlier] for value in found]
        return found

    sent = []
    edges_sent = []
    arrived = [set(), set()]
    done = {}

    def forward(relative, half, step):
        copies = hops(relative, half, step)
        done[(relative ^ 2 ** orders[half][step], half)] = copies
        sent.extend(copies)

    for step in range(steps):
        for half in (0, 1):
            forward(0, half, step)
    if rim:
        edges_sent.extend(edge_hops(0))

    top = width if rim else 0
    middle = tokens // 2

    def place_chunk(slot, parts):
        for index in range(count):

            @pl.when(slot == index)
            def _():
                base = index * chunk
                full[top : top + tokens, base : base + main] = parts[0]
                if kinds > 1:
                    full[top : top + middle, base + main : base + chunk] = parts[1][:, : chunk - main]
                    full[top + middle : top + tokens, base + main : base + chunk] = parts[1][:, chunk - main :]

    def absolute(relative):
        return combined(place, relative, steps)

    place_chunk(place, [ref[...] for ref in owns])

    for step in range(steps):
        for half in (0, 1):
            bit = 2 ** orders[half][step]
            for relative in [value ^ bit for value in reached(half, step)]:
                for copy in done[(relative, half)]:
                    copy.wait_recv()
                arrived[half].add(relative)
                for later in range(step + 1, steps):
                    forward(relative, half, later)
                if relative in arrived[1 - half]:
                    if rim:
                        edges_sent.extend(edge_hops(relative))
                    place_chunk(absolute(relative), [ref[relative] for ref in slots])
    for copy in sent:
        copy.wait_send()
    if rim:
        for copy in edges_sent:
            copy.wait()
        above_scale = (1 - upper).astype(jnp.float32)
        below_scale = upper.astype(jnp.float32)
        for index in range(count):
            slot = combined(place, index, steps)
            values = edges[0][slot].astype(jnp.float32)
            base = index * chunk
            full[0:width, base : base + main] = (values * above_scale).astype(full.dtype)
            full[top + tokens :, base : base + main] = (values * below_scale).astype(full.dtype)
            if kinds > 1:
                values = edges[1][slot].astype(jnp.float32)
                high_lanes, low_lanes = values[:, chunk - main :], values[:, : chunk - main]
                full[0:width, base + main : base + chunk] = (high_lanes * above_scale).astype(full.dtype)
                full[top + tokens :, base + main : base + chunk] = (low_lanes * below_scale).astype(full.dtype)


def gathered(parts, width, rim, number):
    count = lax.axis_size("ch")
    kinds = len(parts)
    tokens = parts[0].shape[0]
    chunk = sum(part.shape[0] * part.shape[1] for part in parts) // tokens
    high = tokens + (2 * width if rim else 0)
    vmem = pl.BlockSpec(memory_space=pltpu.VMEM)
    dma = pltpu.SemaphoreType.DMA
    scratch = [pltpu.VMEM((count, *part.shape), part.dtype) for part in parts]
    if rim:
        scratch = scratch + [pltpu.VMEM((count, width, part.shape[1]), part.dtype) for part in parts]
    scratch = scratch + [dma((kinds, count, 2)), dma((kinds, count, 2))]
    if rim:
        scratch = scratch + [dma((kinds, count)), dma((kinds, count))]
    return pl.pallas_call(
        functools.partial(gather_kernel, count, width, rim, kinds),
        out_shape=jax.ShapeDtypeStruct((high, count * chunk), parts[0].dtype),
        in_specs=[vmem] * kinds,
        out_specs=vmem,
        scratch_shapes=scratch,
        compiler_params=pltpu.CompilerParams(collective_id=number, has_side_effects=True, vmem_limit_bytes=14 * 2**20),
    )(*parts)


def conv_kernel(width, lanes, padded, weight, extra, out, stats, shifted):
    tap = pl.program_id(0)
    high, depth = padded.shape
    tokens = out.shape[0]

    @pl.when(tap == 0)
    def _():
        @pl.loop(0, depth // lanes)
        def _(block):
            span = pl.ds(pl.multiple_of(block * lanes, lanes), lanes)
            value = padded[:, span].astype(jnp.float32)
            column = lax.broadcasted_iota(jnp.int32, value.shape, 0) % width
            before = jnp.where(column == 0, 0.0, pltpu.roll(value, 1, 0))
            after = jnp.where(column == width - 1, 0.0, pltpu.roll(value, high - 1, 0))
            shifted[0, :, span] = before.astype(shifted.dtype)
            shifted[1, :, span] = padded[:, span]
            shifted[2, :, span] = after.astype(shifted.dtype)

    start = pl.multiple_of((tap // 3) * width, width)
    product = right_product(shifted[tap % 3, pl.ds(start, tokens), :], weight[0])

    @pl.when(tap == 0)
    def _():
        out[...] = product + extra[...].astype(jnp.float32)

    @pl.when(tap > 0)
    def _():
        out[...] += product

    @pl.when(tap == pl.num_programs(0) - 1)
    def _():
        value = out[...]
        stats[0:1] = jnp.sum(value, axis=0, keepdims=True)
        stats[1:2] = jnp.sum(value * value, axis=0, keepdims=True)


def conv_taps(padded, weight, extra, width):
    high, depth = padded.shape
    outs = weight.shape[0]
    taps = jnp.transpose(weight, (1, 2, 0, 3)).reshape(-1, outs, depth)
    tokens = high - 2 * width
    count = taps.shape[0]
    return pl.pallas_call(
        functools.partial(conv_kernel, width, 128),
        grid=(count,),
        out_shape=(
            jax.ShapeDtypeStruct((tokens, outs), jnp.float32),
            jax.ShapeDtypeStruct((2, outs), jnp.float32),
        ),
        in_specs=[
            pl.BlockSpec((high, depth), lambda tap: (0, 0)),
            pl.BlockSpec((1, outs, depth), lambda tap: (tap, 0, 0)),
            pl.BlockSpec(extra.shape, lambda tap: (0, 0)),
        ],
        out_specs=(
            pl.BlockSpec((tokens, outs), lambda tap: (0, 0)),
            pl.BlockSpec((2, outs), lambda tap: (0, 0)),
        ),
        scratch_shapes=[pltpu.VMEM((3, high, depth), padded.dtype)],
        compiler_params=pltpu.CompilerParams(vmem_limit_bytes=18 * 2**20),
        cost_estimate=pl.CostEstimate(
            flops=2 * count * tokens * outs * depth, bytes_accessed=count * outs * depth * 2, transcendentals=0
        ),
    )(padded, taps, extra)


def body(
    latent,
    timestep,
    norm_gain_a,
    conv_weight_a,
    time_weight,
    norm_gain_b,
    conv_weight_b,
    norm_gain_c,
    w_query,
    w_key,
    w_value,
    w_out,
):
    rows, width, local_ch = latent.shape
    span = H // rows
    place = lax.axis_index("row")
    image_id = place // span
    group_width = C // GROUPS
    members = float(H * width * group_width)
    tokens = rows * width

    def channel_sums(flat):
        return jnp.stack([jnp.sum(flat, axis=0), jnp.sum(flat * flat, axis=0)])

    def group_norm(flat, channel, gain, active):
        far = swapped(channel, "row", 0)
        return normalized(flat, channel, far, gain, active, group_width, members)

    def convolve(active, weight, extra, number):
        return conv_taps(gathered(active, width, True, number), weight, extra, width)

    image_ids = jnp.arange(timestep.shape[0])
    step_value = jnp.sum(jnp.where(image_ids == image_id, timestep, 0)).astype(jnp.float32)
    half = TDIM // 2
    freqs = jnp.exp(-math.log(10000.0) * jnp.arange(half, dtype=jnp.float32) / half)
    angles = step_value * freqs
    sinus = jnp.concatenate([jnp.cos(angles), jnp.sin(angles)])[None, :].astype(jnp.bfloat16)
    time_add = jax.nn.silu(jnp.dot(sinus, time_weight, preferred_element_type=jnp.float32))
    source = latent.reshape(tokens, local_ch)
    active_a = group_norm(source, channel_sums(source.astype(jnp.float32)), norm_gain_a, True)
    hidden_a, sums_a = convolve(active_a, conv_weight_a, time_add, 0)
    active_b = group_norm(hidden_a, sums_a, norm_gain_b, True)
    hidden_b, sums_b = convolve(active_b, conv_weight_b, source, 1)
    normed = group_norm(hidden_b, sums_b, norm_gain_c, False)
    inner = w_query.shape[0]
    projections = jnp.concatenate([w_query, w_key, w_value], axis=0)
    weight_cols = projections
    mixed = right_product(gathered(normed, width, False, 2), weight_cols)
    query = mixed[:, :inner].astype(jnp.bfloat16)
    keyed = mixed[:, inner : 2 * inner].astype(jnp.bfloat16)
    valued = mixed[:, 2 * inner :].astype(jnp.bfloat16)
    key_value = jnp.stack([keyed, valued])
    key_value = jnp.concatenate([key_value, swapped(key_value, "row", 0)], axis=1)
    local_heads = inner // HEAD_DIM
    query_heads = query.reshape(tokens, local_heads, HEAD_DIM)
    key_heads = key_value[0].reshape(-1, local_heads, HEAD_DIM)
    value_heads = key_value[1].reshape(-1, local_heads, HEAD_DIM)
    scores = jnp.einsum(
        "qhd,khd->hqk", query_heads, key_heads, preferred_element_type=jnp.float32
    ) * (1.0 / math.sqrt(HEAD_DIM))
    highest = jnp.max(scores, axis=-1, keepdims=True)
    raised = jnp.exp(scores - highest)
    weights = (raised / jnp.sum(raised, axis=-1, keepdims=True)).astype(jnp.bfloat16)
    heads_out = jnp.einsum("hqk,khd->qhd", weights, value_heads, preferred_element_type=jnp.float32)
    heads_out = heads_out.astype(jnp.bfloat16).reshape(tokens, inner)
    weight_cols = w_out
    projected = right_product(gathered((heads_out,), width, False, 3), weight_cols)
    total = hidden_b + projected
    return total.reshape(rows, width, local_ch).astype(jnp.bfloat16)


def solution(mesh):
    return jax.shard_map(
        body,
        mesh=mesh,
        in_specs=(
            P("row", None, "ch"),
            P(),
            P("ch"),
            P("ch", None, None, None),
            P(None, "ch"),
            P("ch"),
            P("ch", None, None, None),
            P("ch"),
            P("ch", None),
            P("ch", None),
            P("ch", None),
            P("ch", None),
        ),
        out_specs=P("row", None, "ch"),
        check_vma=False,
    )
```

```python
import functools
import math

import jax
import jax.numpy as jnp
from jax import lax
from jax.experimental import pallas as pl
from jax.experimental.pallas import tpu as pltpu
from jax.sharding import PartitionSpec as P

C = 1280
GROUPS = 32
HEAD_DIM = 64
TDIM = 320
H = 32


eps_value = 1e-06
MESH = pl.DeviceIdType.MESH


def swapped(value, axis, stride):
    mask = 2**stride
    pairs = [(source, source ^ mask) for source in range(lax.axis_size(axis))]
    return lax.ppermute(value, axis, pairs)


def right_product(left, weight):
    return lax.dot_general(
        left, weight, (((1,), (1,)), ((), ())), preferred_element_type=jnp.float32
    )


def flipped(place, bit):
    return place + bit * (1 - 2 * ((place // bit) % 2))


def combined(place, other, steps):
    total = 0
    for step in range(steps):
        bit = 2**step
        total = total + bit * (((place // bit) + (other // bit)) % 2)
    return total


def norm_kernel(active, block, group_width, members, *refs):
    value_ref, near, far, gain = refs[:4]
    outs = refs[4:]
    tokens, chunk = value_ref.shape
    main = outs[0].shape[1]

    lane_group = lax.broadcasted_iota(jnp.int32, (chunk, chunk), 1) // group_width
    depth_group = lax.broadcasted_iota(jnp.int32, (chunk, chunk), 0) // group_width
    same = jnp.where(lane_group == depth_group, 1.0, 0.0)
    stats = jnp.dot(
        near[...] + far[...], same, precision=lax.Precision.HIGHEST, preferred_element_type=jnp.float32
    )
    mean = stats[0:1] / members
    spread = stats[1:2] / members - mean * mean
    factor = lax.rsqrt(spread + eps_value)
    gains = gain[...]

    def scaled(span):
        value = value_ref[span, :].astype(jnp.float32)
        value = (value - mean) * factor * gains
        if active:
            value = jax.nn.silu(value)
        return value.astype(jnp.bfloat16)

    for step in range(tokens // (2 * block)):
        first = slice(step * block, (step + 1) * block)
        second = slice(tokens // 2 + step * block, tokens // 2 + (step + 1) * block)
        early, late = scaled(first), scaled(second)
        outs[0][first, :] = early[:, :main]
        outs[0][second, :] = late[:, :main]
        if len(outs) > 1:
            outs[1][first, :] = jnp.concatenate([early[:, main:], late[:, main:]], axis=1)


def normalized(value, near, far, gain, active, group_width, members):
    tokens, chunk = value.shape
    tail = chunk % 128 == 64 and chunk > 128
    vmem = pl.BlockSpec(memory_space=pltpu.VMEM)
    shapes = [jax.ShapeDtypeStruct((tokens, chunk - (64 if tail else 0)), jnp.bfloat16)]
    if tail:
        shapes = shapes + [jax.ShapeDtypeStruct((tokens // 2, 128), jnp.bfloat16)]
    return pl.pallas_call(
        functools.partial(norm_kernel, active, 64, group_width, members),
        out_shape=tuple(shapes),
        in_specs=[vmem] * 4,
        out_specs=tuple([vmem] * len(shapes)),
        compiler_params=pltpu.CompilerParams(vmem_limit_bytes=10 * 2**20),
    )(value, near, far, gain[None])


def gather_kernel(count, width, rim, kinds, *refs):
    owns, refs = refs[:kinds], refs[kinds:]
    full, refs = refs[0], refs[1:]
    slots, refs = refs[:kinds], refs[kinds:]
    if rim:
        edges, refs = refs[:kinds], refs[kinds:]
        send_sem, recv_sem, edge_send, edge_recv = refs
    else:
        send_sem, recv_sem = refs
    place = lax.axis_index("ch")
    row = lax.axis_index("row")
    steps = count.bit_length() - 1
    tokens = owns[0].shape[0]
    main = owns[0].shape[1]
    chunk = full.shape[1] // count
    partner = {"row": flipped(row, 1)}
    upper = 1 - row % 2

    barrier = pltpu.get_barrier_semaphore()
    for step in range(steps):
        pl.semaphore_signal(barrier, inc=1, device_id={"ch": flipped(place, 2**step)}, device_id_type=MESH)
    if rim:
        pl.semaphore_signal(barrier, inc=1, device_id=partner, device_id_type=MESH)
    pl.semaphore_wait(barrier, steps + (1 if rim else 0))

    orders = (list(range(steps)), list(range(steps))[::-1])

    def hops(relative, half, step):
        bit = 2 ** orders[half][step]
        target = relative ^ bit
        copies = []
        for kind in range(kinds):
            part = owns[kind].shape[0] // 2
            span = pl.ds(half * part, part)
            source = owns[kind].at[span] if relative == 0 else slots[kind].at[relative, span]
            copy = pltpu.make_async_remote_copy(
                src_ref=source,
                dst_ref=slots[kind].at[target, span],
                send_sem=send_sem.at[kind, target, half],
                recv_sem=recv_sem.at[kind, target, half],
                device_id={"ch": flipped(place, bit)},
                device_id_type=MESH,
            )
            copy.start()
            copies.append(copy)
        return copies

    def edge_hops(relative):
        copies = []
        for kind in range(kinds):
            begin = pl.multiple_of(upper * (owns[kind].shape[0] - width), width)
            span = pl.ds(begin, width)
            source = owns[kind].at[span] if relative == 0 else slots[kind].at[relative, span]
            copy = pltpu.make_async_remote_copy(
                src_ref=source,
                dst_ref=edges[kind].at[relative],
                send_sem=edge_send.at[kind, relative],
                recv_sem=edge_recv.at[kind, relative],
                device_id=partner,
                device_id_type=MESH,
            )
            copy.start()
            copies.append(copy)
        return copies

    def reached(half, step):
        found = [0]
        for earlier in range(step):
            found = found + [value ^ 2 ** orders[half][earlier] for value in found]
        return found

    sent = []
    edges_sent = []
    arrived = [set(), set()]
    done = {}

    def forward(relative, half, step):
        copies = hops(relative, half, step)
        done[(relative ^ 2 ** orders[half][step], half)] = copies
        sent.extend(copies)

    for step in range(steps):
        for half in (0, 1):
            forward(0, half, step)
    if rim:
        edges_sent.extend(edge_hops(0))

    top = width if rim else 0
    middle = tokens // 2

    def place_chunk(slot, parts):
        for index in range(count):

            @pl.when(slot == index)
            def _():
                base = index * chunk
                full[top : top + tokens, base : base + main] = parts[0]
                if kinds > 1:
                    full[top : top + middle, base + main : base + chunk] = parts[1][:, : chunk - main]
                    full[top + middle : top + tokens, base + main : base + chunk] = parts[1][:, chunk - main :]

    def absolute(relative):
        return combined(place, relative, steps)

    place_chunk(place, [ref[...] for ref in owns])

    for step in range(steps):
        for half in (0, 1):
            bit = 2 ** orders[half][step]
            for relative in [value ^ bit for value in reached(half, step)]:
                for copy in done[(relative, half)]:
                    copy.wait_recv()
                arrived[half].add(relative)
                for later in range(step + 1, steps):
                    forward(relative, half, later)
                if relative in arrived[1 - half]:
                    if rim:
                        edges_sent.extend(edge_hops(relative))
                    place_chunk(absolute(relative), [ref[relative] for ref in slots])
    for copy in sent:
        copy.wait_send()
    if rim:
        for copy in edges_sent:
            copy.wait()
        above_scale = (1 - upper).astype(jnp.float32)
        below_scale = upper.astype(jnp.float32)
        for index in range(count):
            slot = combined(place, index, steps)
            values = edges[0][slot].astype(jnp.float32)
            base = index * chunk
            full[0:width, base : base + main] = (values * above_scale).astype(full.dtype)
            full[top + tokens :, base : base + main] = (values * below_scale).astype(full.dtype)
            if kinds > 1:
                values = edges[1][slot].astype(jnp.float32)
                high_lanes, low_lanes = values[:, chunk - main :], values[:, : chunk - main]
                full[0:width, base + main : base + chunk] = (high_lanes * above_scale).astype(full.dtype)
                full[top + tokens :, base + main : base + chunk] = (low_lanes * below_scale).astype(full.dtype)


def gathered(parts, width, rim, number):
    count = lax.axis_size("ch")
    kinds = len(parts)
    tokens = parts[0].shape[0]
    chunk = sum(part.shape[0] * part.shape[1] for part in parts) // tokens
    high = tokens + (2 * width if rim else 0)
    vmem = pl.BlockSpec(memory_space=pltpu.VMEM)
    dma = pltpu.SemaphoreType.DMA
    scratch = [pltpu.VMEM((count, *part.shape), part.dtype) for part in parts]
    if rim:
        scratch = scratch + [pltpu.VMEM((count, width, part.shape[1]), part.dtype) for part in parts]
    scratch = scratch + [dma((kinds, count, 2)), dma((kinds, count, 2))]
    if rim:
        scratch = scratch + [dma((kinds, count)), dma((kinds, count))]
    return pl.pallas_call(
        functools.partial(gather_kernel, count, width, rim, kinds),
        out_shape=jax.ShapeDtypeStruct((high, count * chunk), parts[0].dtype),
        in_specs=[vmem] * kinds,
        out_specs=vmem,
        scratch_shapes=scratch,
        compiler_params=pltpu.CompilerParams(collective_id=number, has_side_effects=True, vmem_limit_bytes=14 * 2**20),
    )(*parts)


def conv_kernel(width, lanes, padded, weight, extra, out, stats, shifted):
    tap = pl.program_id(0)
    high, depth = padded.shape
    tokens = out.shape[0]

    @pl.when(tap == 0)
    def _():
        @pl.loop(0, depth // lanes)
        def _(block):
            span = pl.ds(pl.multiple_of(block * lanes, lanes), lanes)
            value = padded[:, span].astype(jnp.float32)
            column = lax.broadcasted_iota(jnp.int32, value.shape, 0) % width
            before = jnp.where(column == 0, 0.0, pltpu.roll(value, 1, 0))
            after = jnp.where(column == width - 1, 0.0, pltpu.roll(value, high - 1, 0))
            shifted[0, :, span] = before.astype(shifted.dtype)
            shifted[1, :, span] = padded[:, span]
            shifted[2, :, span] = after.astype(shifted.dtype)

    start = pl.multiple_of(tap * width, width)
    product = right_product(shifted[0, pl.ds(start, tokens), :], weight[0])
    for column in range(1, weight.shape[0]):
        product = product + right_product(shifted[column, pl.ds(start, tokens), :], weight[column])

    @pl.when(tap == 0)
    def _():
        out[...] = product + extra[...].astype(jnp.float32)

    @pl.when(tap > 0)
    def _():
        out[...] += product

    @pl.when(tap == pl.num_programs(0) - 1)
    def _():
        value = out[...]
        stats[0:1] = jnp.sum(value, axis=0, keepdims=True)
        stats[1:2] = jnp.sum(value * value, axis=0, keepdims=True)


def conv_taps(padded, weight, extra, width):
    high, depth = padded.shape
    outs = weight.shape[0]
    taps = jnp.transpose(weight, (1, 2, 0, 3)).reshape(-1, outs, depth)
    tokens = high - 2 * width
    count = taps.shape[0]
    return pl.pallas_call(
        functools.partial(conv_kernel, width, 128),
        grid=(count // 3,),
        out_shape=(
            jax.ShapeDtypeStruct((tokens, outs), jnp.float32),
            jax.ShapeDtypeStruct((2, outs), jnp.float32),
        ),
        in_specs=[
            pl.BlockSpec((high, depth), lambda tap: (0, 0)),
            pl.BlockSpec((3, outs, depth), lambda tap: (tap, 0, 0)),
            pl.BlockSpec(extra.shape, lambda tap: (0, 0)),
        ],
        out_specs=(
            pl.BlockSpec((tokens, outs), lambda tap: (0, 0)),
            pl.BlockSpec((2, outs), lambda tap: (0, 0)),
        ),
        scratch_shapes=[pltpu.VMEM((3, high, depth), padded.dtype)],
        compiler_params=pltpu.CompilerParams(vmem_limit_bytes=22 * 2**20),
        cost_estimate=pl.CostEstimate(
            flops=2 * count * tokens * outs * depth, bytes_accessed=count * outs * depth * 2, transcendentals=0
        ),
    )(padded, taps, extra)


def body(
    latent,
    timestep,
    norm_gain_a,
    conv_weight_a,
    time_weight,
    norm_gain_b,
    conv_weight_b,
    norm_gain_c,
    w_query,
    w_key,
    w_value,
    w_out,
):
    rows, width, local_ch = latent.shape
    span = H // rows
    place = lax.axis_index("row")
    image_id = place // span
    group_width = C // GROUPS
    members = float(H * width * group_width)
    tokens = rows * width

    def channel_sums(flat):
        return jnp.stack([jnp.sum(flat, axis=0), jnp.sum(flat * flat, axis=0)])

    def group_norm(flat, channel, gain, active):
        far = swapped(channel, "row", 0)
        return normalized(flat, channel, far, gain, active, group_width, members)

    def convolve(active, weight, extra, number):
        return conv_taps(gathered(active, width, True, number), weight, extra, width)

    image_ids = jnp.arange(timestep.shape[0])
    step_value = jnp.sum(jnp.where(image_ids == image_id, timestep, 0)).astype(jnp.float32)
    half = TDIM // 2
    freqs = jnp.exp(-math.log(10000.0) * jnp.arange(half, dtype=jnp.float32) / half)
    angles = step_value * freqs
    sinus = jnp.concatenate([jnp.cos(angles), jnp.sin(angles)])[None, :].astype(jnp.bfloat16)
    time_add = jax.nn.silu(jnp.dot(sinus, time_weight, preferred_element_type=jnp.float32))
    source = latent.reshape(tokens, local_ch)
    active_a = group_norm(source, channel_sums(source.astype(jnp.float32)), norm_gain_a, True)
    hidden_a, sums_a = convolve(active_a, conv_weight_a, time_add, 0)
    active_b = group_norm(hidden_a, sums_a, norm_gain_b, True)
    hidden_b, sums_b = convolve(active_b, conv_weight_b, source, 1)
    normed = group_norm(hidden_b, sums_b, norm_gain_c, False)
    inner = w_query.shape[0]
    projections = jnp.concatenate([w_query, w_key, w_value], axis=0)
    weight_cols = projections
    mixed = right_product(gathered(normed, width, False, 2), weight_cols)
    query = mixed[:, :inner].astype(jnp.bfloat16)
    keyed = mixed[:, inner : 2 * inner].astype(jnp.bfloat16)
    valued = mixed[:, 2 * inner :].astype(jnp.bfloat16)
    key_value = jnp.stack([keyed, valued])
    key_value = jnp.concatenate([key_value, swapped(key_value, "row", 0)], axis=1)
    local_heads = inner // HEAD_DIM
    query_heads = query.reshape(tokens, local_heads, HEAD_DIM)
    key_heads = key_value[0].reshape(-1, local_heads, HEAD_DIM)
    value_heads = key_value[1].reshape(-1, local_heads, HEAD_DIM)
    scores = jnp.einsum(
        "qhd,khd->hqk", query_heads, key_heads, preferred_element_type=jnp.float32
    ) * (1.0 / math.sqrt(HEAD_DIM))
    highest = jnp.max(scores, axis=-1, keepdims=True)
    raised = jnp.exp(scores - highest)
    weights = (raised / jnp.sum(raised, axis=-1, keepdims=True)).astype(jnp.bfloat16)
    heads_out = jnp.einsum("hqk,khd->qhd", weights, value_heads, preferred_element_type=jnp.float32)
    heads_out = heads_out.astype(jnp.bfloat16).reshape(tokens, inner)
    weight_cols = w_out
    projected = right_product(gathered((heads_out,), width, False, 3), weight_cols)
    total = hidden_b + projected
    return total.reshape(rows, width, local_ch).astype(jnp.bfloat16)


def solution(mesh):
    return jax.shard_map(
        body,
        mesh=mesh,
        in_specs=(
            P("row", None, "ch"),
            P(),
            P("ch"),
            P("ch", None, None, None),
            P(None, "ch"),
            P("ch"),
            P("ch", None, None, None),
            P("ch"),
            P("ch", None),
            P("ch", None),
            P("ch", None),
            P("ch", None),
        ),
        out_specs=P("row", None, "ch"),
        check_vma=False,
    )
```
